32 devices in a mesh: dp: 2 (over y), expert: 16 (over z, x, core).
Axes of the slice: x: 2, y: 2, z: 4, core: 2. Of those that a mesh axis runs over, the one named last changes fastest.
Arguments:
- tokens: bfloat16 [4096, 2048], P(('dp', 'expert')), may hold values from -6 to 6
- output_gradient: bfloat16 [4096, 2048], P(('dp', 'expert')), may hold values from -6 to 6
- chosen_expert_index: int32 [4096, 6], P(('dp', 'expert')), may hold values from 0 to 15, all different within a row; in each aligned block of 128 rows (0 to 127, 128 to 255, ...) at most 60 rows name the same one
- router_weight: float32 [4096, 6], P(('dp', 'expert')), may hold values from 0.05 to 0.6
- gate_weight: bfloat16 [16, 2048, 704], P('expert'), may hold values from -0.125 to 0.125
- up_weight: bfloat16 [16, 2048, 704], P('expert'), may hold values from -0.125 to 0.125
- down_weight: bfloat16 [16, 704, 2048], P('expert'), may hold values from -0.21875 to 0.21875
- adapter_down_first: float32 [16, 704, 32], P('expert', 'dp'), may hold values from -0.21875 to 0.21875
- adapter_down_second: float32 [16, 32, 2048], P('expert', None, 'dp'), may hold values from -1 to 1
- first_mean_a: float32 [16, 704, 32], P('expert', 'dp'), may hold values from -24 to 24
- squared_mean_a: float32 [16, 704, 32], P('expert', 'dp'), may hold values from 4 to 64
- first_mean_b: float32 [16, 32, 2048], P('expert', None, 'dp'), may hold values from -24 to 24
- squared_mean_b: float32 [16, 32, 2048], P('expert', None, 'dp'), may hold values from 4 to 64
Outputs:
- token_grad: bfloat16 [4096, 2048], P(('dp', 'expert'))
- updated_mean_a: float32 [16, 704, 32], P('expert', 'dp')
- updated_squared_a: float32 [16, 704, 32], P('expert', 'dp')
- adam_delta_first: float32 [16, 704, 32], P('expert', 'dp')
- updated_mean_b: float32 [16, 32, 2048], P('expert', None, 'dp')
- updated_squared_b: float32 [16, 32, 2048], P('expert', None, 'dp')
- adam_delta_second: float32 [16, 32, 2048], P('expert', None, 'dp')
The draws below stay inside these ranges and needn't reach their ends.
Inputs may be any that keep to these rules, and one draw needn't show every extreme that they name: `chosen_expert_index`: each token names 6 different experts. Among the 128 tokens of one device (aligned blocks of 128 rows) no expert is named more than 60 times, and in every draw some device names some expert exactly 60 times.
All inputs are finite; a program needn't handle non-finite values.
Results may differ from the reference program's by a relative error of at most 0.02.
Values may be sent and summed in bfloat16 or wider, within the bound.
No kernel may reach another device: no remote copies, remote signals or barrier semaphores. Data moves between devices by JAX's collectives and lax.ppermute only.
A program may use at most 128 MiB of HBM per device.

```python
import math
import jax
import jax.numpy as jnp
import numpy as np
from jax import lax

HIDDEN_WIDTH = 2048
EXPERT_UNITS = 704
ADAPTER_RANK = 32
TOP = 6
TOK_DEV = 128
EXPERT_TOTAL = 16
TOKENS = 4096
CAP = 60


def level_of(stream_key, extent, pieces, least, high):
    loudness = 1.0
    for position, shards_of in pieces:
        steps = jax.random.uniform(jax.random.fold_in(jax.random.fold_in(stream_key, 6), position), (shards_of,), jnp.float32, least / len(pieces), high / len(pieces))
        loudness = loudness * jnp.repeat(jnp.exp(steps), extent[position] // shards_of).reshape((-1,) + (1,) * (len(extent) - 1 - position))
    return loudness


def assign_block(stream_key, own, number, rows, amount, top, bound, skew):
    order = jax.random.permutation(stream_key, amount)
    heavy_load, usual = shares(amount, rows * top, bound, skew, True), shares(amount, rows * top, bound, skew, False)
    places = jnp.arange(amount)

    def named(sizes, offset_by):
        used = int((sizes > 0).sum())
        fixed = max(1, used // 4)
        moved = fixed + (places - fixed + offset_by * (used - fixed)) % max(1, amount - fixed)
        return jnp.zeros((amount,), jnp.int32).at[order[jnp.where(places < fixed, places, moved)]].set(jnp.asarray(sizes, jnp.int32))

    sizes = jnp.where(number % 4 == 0, named(heavy_load, number // 4), named(usual, number - number // 4 - 1))
    mixed = jax.random.permutation(jax.random.fold_in(own, 3), amount)
    source_of, taker = mixed[0:amount // 2 * 2:2], mixed[1:amount // 2 * 2:2]
    slack = jnp.minimum(sizes[source_of] - 1, bound - sizes[taker]) // 2
    slack = jnp.where((source_of == order[0]) | (taker == order[0]) | (sizes[taker] == 0), 0, jnp.maximum(slack, 0))
    moved = jax.random.randint(jax.random.fold_in(own, 4), (amount // 2,), 0, 1 << 20) % (slack + 1)
    sizes = sizes.at[source_of].add(-moved).at[taker].add(moved)
    labels = jnp.searchsorted(jnp.cumsum(sizes), jnp.arange(rows * top), side="right").astype(jnp.int32)
    listing = labels.reshape(top, rows).T
    listing = listing[jax.random.permutation(jax.random.fold_in(own, 1), rows)]
    offset_by = jax.random.randint(jax.random.fold_in(own, 2), (rows, 1), 0, top)
    return jnp.take_along_axis(listing, (jnp.arange(top)[None, :] + offset_by) % top, axis=1)


def shares(number_of, total, reach, slope, full):
    portions = [(1 << 20) // math.isqrt(standing ** slope) + 1 for standing in range(1, number_of + 1)]
    largest = reach if full else min(reach, max(-(-total // number_of), total * portions[0] // sum(portions)))
    least = 1 if total - largest >= number_of - 1 else 0
    given, spare = [largest] + [least] * (number_of - 1), total - largest - least * (number_of - 1)
    while spare > 0:
        movable = [i for i in range(1, number_of) if given[i] < largest] or [i for i in range(1, number_of) if given[i] < reach]
        whole, left = sum([portions[i] for i in movable]), spare
        for i in movable:
            extra = min(reach - given[i], max(1, left * portions[i] // whole), spare)
            given[i] = given[i] + extra
            spare = spare - extra
    return np.array(given)


def bell_draw(stream_key, extent, deviation, most, cuts=(), held_as=jnp.bfloat16):
    values = jax.random.normal(stream_key, extent, jnp.float32) * deviation
    if len(cuts) > 0:
        values = level_of(stream_key, extent, cuts, -0.22, 0.18) * values
    return jnp.clip(values, min=-most, max=most).astype(held_as)


def setup_inputs(seed: int = 0) -> dict:
    streams_of = jax.random.split(jax.random.key(seed), 14)
    tokens = bell_draw(streams_of[0], (TOKENS, HIDDEN_WIDTH), 1.0, 6.0, ((0, 32),))
    output_gradient = bell_draw(streams_of[1], (TOKENS, HIDDEN_WIDTH), 1.0, 6.0, ((0, 32),))
    chosen_expert_index_keys = jax.random.split(jax.random.fold_in(streams_of[2], 1), TOKENS // TOK_DEV)
    chosen_expert_index_turns = jax.random.permutation(jax.random.fold_in(streams_of[2], 3), TOKENS // TOK_DEV)
    chosen_expert_index = jax.vmap(lambda own, number: assign_block(jax.random.fold_in(streams_of[2], 2), own, number, TOK_DEV, EXPERT_TOTAL, TOP, CAP, 2))(chosen_expert_index_keys, chosen_expert_index_turns).reshape((TOKENS, TOP))
    router_weight = jnp.clip(0.05 + 0.55 * jax.random.uniform(streams_of[3], (TOKENS, TOP), jnp.float32) ** level_of(streams_of[3], (TOKENS, TOP), ((0, 32),), -0.2, 0.2), 0.05, 0.6)
    gate_weight = bell_draw(streams_of[4], (EXPERT_TOTAL, HIDDEN_WIDTH, EXPERT_UNITS), HIDDEN_WIDTH ** -0.5, 0.125, ((0, 16),))
    up_weight = bell_draw(streams_of[5], (EXPERT_TOTAL, HIDDEN_WIDTH, EXPERT_UNITS), HIDDEN_WIDTH ** -0.5, 0.125, ((0, 16),))
    down_weight = bell_draw(streams_of[6], (EXPERT_TOTAL, EXPERT_UNITS, HIDDEN_WIDTH), EXPERT_UNITS ** -0.5, 0.21875, ((0, 16),))
    adapter_down_first = bell_draw(streams_of[7], (EXPERT_TOTAL, EXPERT_UNITS, ADAPTER_RANK), EXPERT_UNITS ** -0.5, 0.21875, ((0, 16), (1, 2)), jnp.float32)
    adapter_down_second = bell_draw(streams_of[8], (EXPERT_TOTAL, ADAPTER_RANK, HIDDEN_WIDTH), ADAPTER_RANK ** -0.5, 1.0, ((0, 16), (2, 2)), jnp.float32)
    first_mean_a = bell_draw(streams_of[9], (EXPERT_TOTAL, EXPERT_UNITS, ADAPTER_RANK), 4.0, 24.0, ((0, 16), (1, 2)), jnp.float32)
    squared_mean_a = jnp.clip(jnp.exp(math.log(64.0) - 2.7725887 * jax.random.uniform(streams_of[10], (EXPERT_TOTAL, EXPERT_UNITS, ADAPTER_RANK), jnp.float32) ** level_of(streams_of[10], (EXPERT_TOTAL, EXPERT_UNITS, ADAPTER_RANK), ((0, 16), (1, 2)), -0.2, 0.2)), 4.0, 64.0)
    first_mean_b = bell_draw(streams_of[11], (EXPERT_TOTAL, ADAPTER_RANK, HIDDEN_WIDTH), 4.0, 24.0, ((0, 16), (2, 2)), jnp.float32)
    squared_mean_b = jnp.clip(jnp.exp(math.log(64.0) - 2.7725887 * jax.random.uniform(streams_of[12], (EXPERT_TOTAL, ADAPTER_RANK, HIDDEN_WIDTH), jnp.float32) ** level_of(streams_of[12], (EXPERT_TOTAL, ADAPTER_RANK, HIDDEN_WIDTH), ((0, 16), (2, 2)), -0.2, 0.2)), 4.0, 64.0)
    return {"tokens": tokens, "output_gradient": output_gradient, "chosen_expert_index": chosen_expert_index, "router_weight": router_weight, "gate_weight": gate_weight, "up_weight": up_weight, "down_weight": down_weight, "adapter_down_first": adapter_down_first, "adapter_down_second": adapter_down_second, "first_mean_a": first_mean_a, "squared_mean_a": squared_mean_a, "first_mean_b": first_mean_b, "squared_mean_b": squared_mean_b}


adapter_scale = 2.0
beta_one = 0.9
beta_two = 0.999
bias_one = 1.0 - math.exp(1000.0 * math.log(0.9))
bias_two = 1.0 - math.exp(1000.0 * math.log(0.999))
adam_eps = 1e-08
weight_decay = 0.1
ref_rows = 1024

def expert_pass(rows_in, row_gradients, gate_mat, up_mat, down_mat, first_adapter, second_adapter):
    contract_trailing = (((1,), (1,)), ((), ()))
    contract_leading = (((0,), (0,)), ((), ()))
    gate_pre = jnp.dot(rows_in, gate_mat, preferred_element_type=jnp.float32)
    up_pre = jnp.dot(rows_in, up_mat, preferred_element_type=jnp.float32)
    sigmoid_gate = jax.nn.sigmoid(gate_pre)
    activated = gate_pre * sigmoid_gate
    expert_activation = (activated * up_pre).astype(jnp.bfloat16)
    narrow_product = jnp.dot(expert_activation, first_adapter, preferred_element_type=jnp.float32).astype(jnp.bfloat16)
    narrow_gradient = lax.dot_general(row_gradients, second_adapter, contract_trailing, preferred_element_type=jnp.float32).astype(jnp.bfloat16)
    activation_gradient = lax.dot_general(row_gradients, down_mat, contract_trailing, preferred_element_type=jnp.float32)
    activation_gradient = activation_gradient + adapter_scale * lax.dot_general(narrow_gradient, first_adapter, contract_trailing, preferred_element_type=jnp.float32)
    gate_grad = (activation_gradient * up_pre * sigmoid_gate * (1.0 + gate_pre * (1.0 - sigmoid_gate))).astype(jnp.bfloat16)
    up_grad = (activation_gradient * activated).astype(jnp.bfloat16)
    input_grad = lax.dot_general(gate_grad, gate_mat, contract_trailing, preferred_element_type=jnp.float32)
    input_grad = (input_grad + lax.dot_general(up_grad, up_mat, contract_trailing, preferred_element_type=jnp.float32)).astype(jnp.bfloat16)
    first_factor_gradient = adapter_scale * lax.dot_general(expert_activation, narrow_gradient, contract_leading, preferred_element_type=jnp.float32)
    second_factor_gradient = adapter_scale * lax.dot_general(narrow_product, row_gradients, contract_leading, preferred_element_type=jnp.float32)
    return (input_grad, first_factor_gradient, second_factor_gradient)

def decoupled_adam_update(param, grad, moment, second):
    moment_new = beta_one * moment + (1.0 - beta_one) * grad
    second_new = beta_two * second + (1.0 - beta_two) * grad * grad
    update = moment_new / bias_one / (jnp.sqrt(second_new / bias_two) + adam_eps) + weight_decay * param
    return (moment_new, second_new, update)

def reference(tokens, output_gradient, chosen_expert_index, router_weight, gate_weight, up_weight, down_weight, adapter_down_first, adapter_down_second, first_mean_a, squared_mean_a, first_mean_b, squared_mean_b):
    pair_total = TOKENS * TOP
    chosen = chosen_expert_index.reshape(-1).astype(jnp.int32)
    sorted_pairs = jnp.argsort(chosen, stable=True).astype(jnp.int32)
    expert_load = jnp.zeros((EXPERT_TOTAL,), jnp.int32).at[chosen].add(1)
    first_row = (jnp.cumsum(expert_load) - expert_load).astype(jnp.int32)
    pair_weight = router_weight.reshape(-1)
    first_adapter = adapter_down_first.astype(jnp.bfloat16)
    second_adapter = adapter_down_second.astype(jnp.bfloat16)

    def per_expert(grad_sum, expert):
        gate_mat = lax.dynamic_index_in_dim(gate_weight, expert, 0, keepdims=False)
        up_mat = lax.dynamic_index_in_dim(up_weight, expert, 0, keepdims=False)
        down_mat = lax.dynamic_index_in_dim(down_weight, expert, 0, keepdims=False)
        factor_a = lax.dynamic_index_in_dim(first_adapter, expert, 0, keepdims=False)
        factor_b = lax.dynamic_index_in_dim(second_adapter, expert, 0, keepdims=False)
        row_count = expert_load[expert]
        row_first = first_row[expert]
        block_total = (row_count + ref_rows - 1) // ref_rows

        def one_block(block_index, running):
            grad_acc, total_a, total_b = running
            offsets = (block_index * ref_rows + jnp.arange(ref_rows, dtype=jnp.int32)).astype(jnp.int32)
            valid_row = offsets < row_count
            pair_index = sorted_pairs[jnp.clip(row_first + offsets, 0, pair_total - 1).astype(jnp.int32)]
            token_index = (pair_index // TOP).astype(jnp.int32)
            rows_in = jnp.where(valid_row[:, None], tokens[token_index], jnp.zeros((), tokens.dtype))
            scaled = pair_weight[pair_index][:, None] * output_gradient[token_index].astype(jnp.float32)
            row_gradients = jnp.where(valid_row[:, None], scaled, jnp.zeros((), jnp.float32)).astype(jnp.bfloat16)
            input_grad, part_a, part_b = expert_pass(rows_in, row_gradients, gate_mat, up_mat, down_mat, factor_a, factor_b)
            masked = jnp.where(valid_row[:, None], input_grad.astype(jnp.float32), jnp.zeros((), jnp.float32))
            grad_acc = grad_acc.at[token_index].add(masked)
            return (grad_acc, total_a + part_a, total_b + part_b)
        start_state = (grad_sum, jnp.zeros((EXPERT_UNITS, ADAPTER_RANK), jnp.float32), jnp.zeros((ADAPTER_RANK, HIDDEN_WIDTH), jnp.float32))
        grad_sum, total_a, total_b = lax.fori_loop(0, block_total, one_block, start_state)
        return (grad_sum, (total_a, total_b))
    grad_sum, (first_factor_gradient, second_factor_gradient) = lax.scan(per_expert, jnp.zeros((TOKENS, HIDDEN_WIDTH), jnp.float32), jnp.arange(EXPERT_TOTAL, dtype=jnp.int32))
    token_grad = grad_sum.astype(jnp.bfloat16)
    updated_mean_a, updated_squared_a, adam_delta_first = decoupled_adam_update(adapter_down_first, first_factor_gradient, first_mean_a, squared_mean_a)
    updated_mean_b, updated_squared_b, adam_delta_second = decoupled_adam_update(adapter_down_second, second_factor_gradient, first_mean_b, squared_mean_b)
    return (token_grad, updated_mean_a, updated_squared_a, adam_delta_first, updated_mean_b, updated_squared_b, adam_delta_second)
```

```python
import functools
import math

import jax
import jax.numpy as jnp
from jax import lax
from jax.experimental import pallas as pl
from jax.experimental.pallas import tpu as pltpu
from jax.sharding import PartitionSpec as P

adapter_scale = 2.0
beta_one = 0.9
beta_two = 0.999
bias_one = 1.0 - math.exp(1000.0 * math.log(0.9))
bias_two = 1.0 - math.exp(1000.0 * math.log(0.999))
adam_eps = 1e-08
weight_decay = 0.1


META_ROWS = 8
FIELDS = 4
NT = (((1,), (1,)), ((), ()))
TN = (((0,), (0,)), ((), ()))
NN = (((1,), (0,)), ((), ()))


def dot32(a, b, dims):
    return lax.dot_general(a, b, dims, preferred_element_type=jnp.float32)


def prep_kernel(experts, chosen_ref, weight_ref, tokens_ref, out_ref):
    top, count = chosen_ref.shape
    width = tokens_ref.shape[1]
    per_row = width // count
    ids = lax.broadcasted_iota(jnp.int32, (experts, count), 0)
    named = jnp.zeros((experts, count), jnp.float32)
    weight = jnp.zeros((experts, count), jnp.float32)
    for k in range(top):
        hit = chosen_ref[k : k + 1, :] == ids
        named = jnp.where(hit, 1.0, named)
        weight = jnp.where(hit, weight_ref[k : k + 1, :], weight)
    before = lax.broadcasted_iota(jnp.int32, (count, count), 0) < lax.broadcasted_iota(
        jnp.int32, (count, count), 1
    )
    rank = dot32(named.astype(jnp.bfloat16), before.astype(jnp.bfloat16), NN)
    rank = jnp.where(named > 0.0, rank, -1.0)
    high = weight.astype(jnp.bfloat16).astype(jnp.float32)
    middle = (weight - high).astype(jnp.bfloat16).astype(jnp.float32)
    low = weight - high - middle
    groups = []
    for first in range(0, experts, per_row):
        for field in (rank, high, middle, low):
            last = min(first + per_row, experts)
            line = [field[e : e + 1, :] for e in range(first, last)]
            if last - first < per_row:
                line.append(jnp.zeros((1, width - (last - first) * count), jnp.float32))
            groups.append(jnp.concatenate(line, axis=1))
    if len(groups) < META_ROWS:
        groups.append(jnp.zeros((META_ROWS - len(groups), width), jnp.float32))
    out_ref[0:count, :] = tokens_ref[...]
    out_ref[count : count + META_ROWS, :] = jnp.concatenate(groups, axis=0).astype(jnp.bfloat16)


def prepare(experts, chosen, weight, tokens):
    count, width = tokens.shape
    return pl.pallas_call(
        functools.partial(prep_kernel, experts),
        out_shape=jax.ShapeDtypeStruct((count + META_ROWS, width), jnp.bfloat16),
        name="prepare",
    )(chosen.T, weight.T, tokens)


def block_kernel(
    slots,
    scalars_ref,
    tok0_ref,
    tok1_ref,
    grd0_ref,
    grd1_ref,
    gate0_ref,
    up0_ref,
    down0_ref,
    gate1_ref,
    up1_ref,
    down1_ref,
    a_ref,
    b_ref,
    part0_ref,
    part1_ref,
    ga_ref,
    gb_ref,
    tok_buf,
    grd_buf,
    w_buf,
    acc_buf,
    data_sem,
    w_sem,
):
    count, width = grd0_ref.shape
    per_row = width // count
    weights = ((gate0_ref, up0_ref, down0_ref), (gate1_ref, up1_ref, down1_ref))
    any_valid = scalars_ref[1] > 0

    @pl.when(jnp.logical_not(any_valid))
    def _():
        ga_ref[...] = jnp.zeros_like(ga_ref)
        gb_ref[...] = jnp.zeros_like(gb_ref)

    @pl.when(any_valid)
    def _():
        data = [
            pltpu.make_async_copy(tok0_ref, tok_buf.at[0], data_sem.at[0]),
            pltpu.make_async_copy(tok1_ref, tok_buf.at[1], data_sem.at[1]),
            pltpu.make_async_copy(grd0_ref, grd_buf.at[0], data_sem.at[2]),
            pltpu.make_async_copy(grd1_ref, grd_buf.at[1], data_sem.at[3]),
        ]
        for c in data:
            c.start()
        loads = []
        for j in range(2):
            for m in (0, 1, 2):
                c = pltpu.make_async_copy(weights[j][m], w_buf.at[j, m], w_sem.at[j, m])
                c.start()
                loads.append(c)
        for c in data:
            c.wait()
        row_ids = lax.broadcasted_iota(jnp.int32, (META_ROWS, count), 0)
        slot_ids = lax.broadcasted_iota(jnp.int32, (slots, count), 0).astype(jnp.float32)
        for j in range(2):
            expert = scalars_ref[0] if j == 0 else scalars_ref[0] + 1 - 2 * (scalars_ref[0] % 2)
            column = pl.multiple_of((expert % per_row) * count, count)
            first = (expert // per_row) * FIELDS
            picks = []
            rows = []
            grads = []
            for s in range(2):
                meta = tok_buf[s, count : count + META_ROWS, pl.ds(column, count)].astype(jnp.float32)

                def field(f):
                    return jnp.sum(jnp.where(row_ids == first + f, meta, 0.0), axis=0, keepdims=True)

                hit = slot_ids == field(0)
                weight = field(1) + field(2) + field(3)
                weight_col = jnp.sum(jnp.where(hit, weight, 0.0), axis=1, keepdims=True)
                pick = hit.astype(jnp.bfloat16)
                picks.append(pick)
                rows.append(dot32(pick, tok_buf[s, 0:count, :], NN).astype(jnp.bfloat16))
                grads.append((weight_col * dot32(pick, grd_buf[s], NN)).astype(jnp.bfloat16))
            rows_in = jnp.concatenate(rows, axis=0)
            row_grad = jnp.concatenate(grads, axis=0)
            factor_a = a_ref[j]
            factor_b = b_ref[j]
            low_grad = dot32(row_grad, factor_b, NT).astype(jnp.bfloat16)
            loads[3 * j].wait()
            gate_pre = dot32(rows_in, w_buf[j, 0], NT)
            loads[3 * j + 1].wait()
            up_pre = dot32(rows_in, w_buf[j, 1], NT)
            sig = jax.nn.sigmoid(gate_pre)
            act = gate_pre * sig
            hidden = (act * up_pre).astype(jnp.bfloat16)
            low_rank = dot32(hidden, factor_a, NT).astype(jnp.bfloat16)
            loads[3 * j + 2].wait()
            hidden_grad = dot32(row_grad, w_buf[j, 2], NT)
            hidden_grad = hidden_grad + adapter_scale * dot32(low_grad, factor_a, NN)
            gate_grad = (hidden_grad * up_pre * sig * (1.0 + gate_pre * (1.0 - sig))).astype(jnp.bfloat16)
            up_grad = (hidden_grad * act).astype(jnp.bfloat16)
            ga_ref[j] = adapter_scale * dot32(low_grad, hidden, TN)
            gb_ref[j] = adapter_scale * dot32(low_rank, row_grad, TN)
            pair_grad = (dot32(gate_grad, w_buf[j, 0], NN) + dot32(up_grad, w_buf[j, 1], NN)).astype(
                jnp.bfloat16
            )
            for s in range(2):
                back = dot32(picks[s], pair_grad[s * slots : (s + 1) * slots, :], TN)
                if j == 0:
                    acc_buf[s] = back
                else:
                    (part0_ref, part1_ref)[s][...] = (acc_buf[s] + back).astype(jnp.bfloat16)


def run_blocks(slots, scalars, tok0, tok1, grd0, grd1, own, other, fac_a, fac_b):
    count, width = grd0.shape
    units = own[0].shape[0]
    rank = fac_a.shape[1]
    hbm = pl.BlockSpec(memory_space=pl.ANY)
    vmem = pl.BlockSpec(memory_space=pltpu.VMEM)
    rows = 4 * slots
    return pl.pallas_call(
        functools.partial(block_kernel, slots),
        out_shape=(
            jax.ShapeDtypeStruct((count, width), jnp.bfloat16),
            jax.ShapeDtypeStruct((count, width), jnp.bfloat16),
            jax.ShapeDtypeStruct((2, rank, units), jnp.float32),
            jax.ShapeDtypeStruct((2, rank, width), jnp.float32),
        ),
        in_specs=[pl.BlockSpec(memory_space=pltpu.SMEM)] + [hbm] * 10 + [vmem] * 2,
        out_specs=[vmem] * 4,
        scratch_shapes=[
            pltpu.VMEM((2,) + tok0.shape, jnp.bfloat16),
            pltpu.VMEM((2, count, width), jnp.bfloat16),
            pltpu.VMEM((2, 3, units, width), jnp.bfloat16),
            pltpu.VMEM((2, count, width), jnp.float32),
            pltpu.SemaphoreType.DMA((4,)),
            pltpu.SemaphoreType.DMA((2, 3)),
        ],
        cost_estimate=pl.CostEstimate(
            flops=12 * rows * units * width,
            bytes_accessed=12 * units * width + 16 * count * width,
            transcendentals=rows * units,
        ),
        compiler_params=pltpu.CompilerParams(vmem_limit_bytes=48 * 1024 * 1024),
        name="blocks",
    )(scalars, tok0, tok1, grd0, grd1, *own, *other, fac_a, fac_b)


def decoupled_adam_update(param, grad, moment, second):
    moment_new = beta_one * moment + (1.0 - beta_one) * grad
    second_new = beta_two * second + (1.0 - beta_two) * grad * grad
    update = (
        moment_new / bias_one / (jnp.sqrt(second_new / bias_two) + adam_eps) + weight_decay * param
    )
    return (moment_new, second_new, update)


def add_rounded(*terms):
    total = terms[0].astype(jnp.float32)
    for t in terms[1:]:
        total = total + t.astype(jnp.float32)
    return total.astype(jnp.bfloat16)


def shards(
    tokens,
    output_gradient,
    chosen_expert_index,
    router_weight,
    gate_weight,
    up_weight,
    down_weight,
    adapter_down_first,
    adapter_down_second,
    first_mean_a,
    squared_mean_a,
    first_mean_b,
    squared_mean_b,
):
    token_count, model_width = tokens.shape
    top_count = chosen_expert_index.shape[1]
    experts = lax.axis_size("expert")
    replicas = lax.axis_size("dp")
    capacity = min(token_count, 5 * token_count * top_count // (4 * experts))
    slots = -(-capacity // 16) * 16
    depth = experts // 4
    me = lax.axis_index("expert")
    my_z = me // 4
    my_dp = lax.axis_index("dp")

    def permute(v, pairs):
        return lax.ppermute(v, "expert", pairs)

    every = range(experts)
    core_pairs = [(i, i ^ 1) for i in every]
    x_pairs = [(i, i ^ 2) for i in every]

    def x_up(k):
        return [(i, i ^ 2) for i in every if i // 4 >= k]

    def x_down(k):
        return [(i, i ^ 2) for i in every if i // 4 < depth - k]

    def z_up(k):
        return [(i, i + 4) for i in every if k - 1 <= i // 4 < depth - 1]

    def z_down(k):
        return [(i, i - 4) for i in every if 1 <= i // 4 <= depth - k]

    def back_up(k):
        return [(i, i + 4) for i in every if i // 4 <= depth - 1 - k]

    def back_down(k):
        return [(i, i - 4) for i in every if i // 4 >= k]

    grd = output_gradient
    tok = prepare(experts, chosen_expert_index, router_weight, tokens)

    grd_x, tok_x = permute(grd, x_pairs), permute(tok, x_pairs)
    up_t, up_g, down_t, down_g = [tok], [grd], [tok], [grd]
    xup_t, xup_g, xdown_t, xdown_g = [None], [None], [None], [None]
    for k in range(1, depth):
        up_g.append(permute(up_g[-1], z_up(k)))
        down_g.append(permute(down_g[-1], z_down(k)))
        up_t.append(permute(up_t[-1], z_up(k)))
        down_t.append(permute(down_t[-1], z_down(k)))
        xup_g.append(permute(up_g[k], x_up(k)))
        xdown_g.append(permute(down_g[k], x_down(k)))
        xup_t.append(permute(up_t[k], x_up(k)))
        xdown_t.append(permute(down_t[k], x_down(k)))

    own = (gate_weight[0].T, up_weight[0].T, down_weight[0])
    other = tuple(permute(w, core_pairs) for w in own)

    shard_units = adapter_down_first.shape[1]
    packed = jnp.concatenate(
        [adapter_down_first[0].T.astype(jnp.bfloat16), adapter_down_second[0].astype(jnp.bfloat16)],
        axis=1,
    )
    pieces = jnp.zeros((replicas,) + packed.shape, jnp.bfloat16)
    pieces = lax.dynamic_update_slice_in_dim(pieces, packed[None], my_dp, 0)
    for s in range(1, replicas):
        got = lax.ppermute(packed, "dp", [(i, (i + s) % replicas) for i in range(replicas)])
        pieces = lax.dynamic_update_slice_in_dim(pieces, got[None], (my_dp - s) % replicas, 0)
    both = jnp.stack([pieces, permute(pieces, core_pairs)])
    full = both.transpose(0, 2, 1, 3)
    rank = packed.shape[0]
    fac_a = full[..., :shard_units].reshape(2, rank, -1)
    fac_b = full[..., shard_units:].reshape(2, rank, -1)

    def blocks(valid, t0, t1, g0, g1):
        scalars = jnp.stack([me, valid]).astype(jnp.int32)
        return run_blocks(slots, scalars, t0, t1, g0, g1, own, other, fac_a, fac_b)

    mine, theirs, sum_a, sum_b = blocks(jnp.int32(1), tok, tok_x, grd, grd_x)
    centre = add_rounded(mine, permute(theirs, x_pairs))
    to_down, to_up = [None], [None]
    for k in range(1, depth):
        valid = jnp.logical_or(my_z >= k, my_z < depth - k)
        p_down, p_up, ga, gb = blocks(valid, up_t[k], down_t[k], up_g[k], down_g[k])
        sum_a, sum_b = sum_a + ga, sum_b + gb
        q_down, q_up, ga, gb = blocks(valid, xup_t[k], xdown_t[k], xup_g[k], xdown_g[k])
        sum_a, sum_b = sum_a + ga, sum_b + gb
        to_down.append(add_rounded(p_down, permute(q_down, x_up(k))))
        to_up.append(add_rounded(p_up, permute(q_up, x_down(k))))

    from_below, from_above = None, None
    for k in range(depth - 1, 0, -1):
        send_up, send_down = to_up[k], to_down[k]
        if from_below is not None:
            send_up = add_rounded(send_up, from_below)
            send_down = add_rounded(send_down, from_above)
        from_below = permute(send_up, back_up(k))
        from_above = permute(send_down, back_down(k))
    token_grad = add_rounded(centre, from_below, from_above) if depth > 1 else centre

    packed_grad = jnp.concatenate(
        [
            sum_a.reshape(2, rank, replicas, shard_units),
            sum_b.reshape(2, rank, replicas, -1),
        ],
        axis=3,
    ).transpose(0, 2, 1, 3)
    total = packed_grad[0] + permute(packed_grad[1], core_pairs)
    grad = lax.dynamic_index_in_dim(total, my_dp, 0, keepdims=False)
    for s in range(1, replicas):
        part = lax.dynamic_index_in_dim(total, (my_dp + s) % replicas, 0, keepdims=False)
        grad = grad + lax.ppermute(part, "dp", [(i, (i + s) % replicas) for i in range(replicas)])
    grad_a = grad[:, :shard_units].T
    grad_b = grad[:, shard_units:]
    updated_mean_a, updated_squared_a, adam_delta_first = decoupled_adam_update(
        adapter_down_first[0], grad_a, first_mean_a[0], squared_mean_a[0]
    )
    updated_mean_b, updated_squared_b, adam_delta_second = decoupled_adam_update(
        adapter_down_second[0], grad_b, first_mean_b[0], squared_mean_b[0]
    )
    return (
        token_grad,
        updated_mean_a[None],
        updated_squared_a[None],
        adam_delta_first[None],
        updated_mean_b[None],
        updated_squared_b[None],
        adam_delta_second[None],
    )


def solution(mesh):
    rows = P(("dp", "expert"), None)
    whole = P("expert", None, None)
    placed_a = P("expert", "dp", None)
    placed_b = P("expert", None, "dp")
    return jax.shard_map(
        shards,
        mesh=mesh,
        in_specs=(rows,) * 4
        + (whole,) * 3
        + (placed_a, placed_b, placed_a, placed_a, placed_b, placed_b),
        out_specs=(rows,) + (placed_a,) * 3 + (placed_b,) * 3,
        check_vma=False,
    )
```
